32 devices in a mesh: rows: 16 (over z, x, core), freq: 2 (over y).
Axes of the slice: x: 2, y: 2, z: 4, core: 2. Of those that a mesh axis runs over, the one named last changes fastest.
Arguments:
- design: float32 [128, 65536], P('rows'), may hold values from 0.05 to 0.95
- passive: int32 [128, 65536], P('rows'), may hold values 0 or 1
- state: bfloat16 [2, 2, 128, 65536], P(None, 'freq', 'rows'), may hold values from -36 to 36
- adjoint: bfloat16 [2, 2, 128, 65536], P(None, 'freq', 'rows'), may hold values from -36 to 36
- omega_sq: float32 [2], replicated, may hold values from 0.05 to 2
- assign: int32 [2], P('freq'), may hold values from 0 to 1, each once
Outputs:
- gradient: float32 [128, 65536], P('rows')
The draws below stay inside these ranges and needn't reach their ends.
Inputs may be any that keep to these rules, and one draw needn't show every extreme that they name: `assign`: each of 0 .. 1 appears once.
All inputs are finite; a program needn't handle non-finite values. No bound on the sum of `passive` on one device may be relied on, other than what follows from the above.
Results may differ from the reference program's by a relative error of at most 0.0003.
Values may be sent and summed in bfloat16 or wider, within the bound.
A program may use at most 128 MiB of HBM per device.

```python
import math
import jax
import jax.numpy as jnp
from jax import lax

NC = 65536
RADIUS = 8
NR = 128
NF = 2


def field_draw(key, salt):
    base_key, col_key = jax.random.split(jax.random.fold_in(key, salt))
    rows = jnp.arange(NR, dtype=jnp.float32) / max(NR - 1, 1)
    col_scale = jnp.exp(math.log(3.0) * jax.random.uniform(col_key, (NC,), jnp.float32))
    values = jnp.clip(jax.random.normal(base_key, (2, NF, NR, NC), jnp.float32), -4.0, 4.0)
    row_scale = jnp.exp(math.log(3.0) * rows)
    return (values * row_scale[None, None, :, None] * col_scale).astype(jnp.bfloat16)


def draw_state(key, part):
    return field_draw(key, 11)


def draw_adjoint(key, part):
    return field_draw(key, 23)


def draw_design(key, part):
    wave_key, phase_key, noise_key = jax.random.split(jax.random.fold_in(key, 31), 3)
    waves = jax.random.uniform(wave_key, (2,), jnp.float32, 1.0, 4.0)
    phases = jax.random.uniform(phase_key, (2,), jnp.float32, 0.0, 2.0 * math.pi)
    rows = jnp.arange(NR, dtype=jnp.float32) / NR
    cols = jnp.arange(NC, dtype=jnp.float32) / NC
    amplitude = 0.3
    rough = 0.15
    smooth = jnp.sin(2.0 * math.pi * waves[0] * rows + phases[0])[:, None] * jnp.cos(2.0 * math.pi * waves[1] * cols + phases[1])[None, :]
    noise = jax.random.uniform(noise_key, (NR, NC), jnp.float32, -rough, rough)
    return 0.5 + amplitude * smooth + noise


def set_ends(values, own_key, smallest, largest):
    shape = values.shape
    place = [jax.random.randint(jax.random.fold_in(own_key, axis), (), 0, shape[axis]) for axis in range(len(shape))]
    values = values.at[tuple(place)].set(smallest)
    longest = shape.index(max(shape))
    place[longest] = (place[longest] + 1) % shape[longest]
    return values.at[tuple(place)].set(largest)


def setup_inputs(seed: int = 0) -> dict:
    keys = jax.random.split(jax.random.key(seed), 7)
    return {
        "design": draw_design(jax.random.fold_in(keys[6], 71), 0),
        "passive": set_ends((jax.random.randint(keys[1], (NR, NC), 0, 8) < 1).astype(jnp.int32), jax.random.fold_in(keys[1], 1), 0, 1),
        "state": draw_state(jax.random.fold_in(keys[6], 71), 0),
        "adjoint": draw_adjoint(jax.random.fold_in(keys[6], 71), 0),
        "omega_sq": jnp.clip(jnp.exp(jax.random.uniform(keys[4], (NF,), jnp.float32, math.log(0.05), math.log(2.0))), 0.05, 2.0),
        "assign": jax.random.permutation(keys[5], NF).astype(jnp.int32),
    }


sharpness = 8.0
threshold = 0.5
exponent = 3.0
soft_floor = 0.001
loss_factor = 0.2
epsilon = 1e-06
stiff_table = [[4.0 / 6, -1.0 / 6, -1.0 / 6, -2.0 / 6], [-1.0 / 6, 4.0 / 6, -2.0 / 6, -1.0 / 6], [-1.0 / 6, -2.0 / 6, 4.0 / 6, -1.0 / 6], [-2.0 / 6, -1.0 / 6, -1.0 / 6, 4.0 / 6]]
mass_table = [[4.0 / 36, 2.0 / 36, 2.0 / 36, 1.0 / 36], [2.0 / 36, 4.0 / 36, 1.0 / 36, 2.0 / 36], [2.0 / 36, 1.0 / 36, 4.0 / 36, 2.0 / 36], [1.0 / 36, 2.0 / 36, 2.0 / 36, 4.0 / 36]]

def tap_list():
    return [float(RADIUS + 1 - abs(offset)) for offset in range(-RADIUS, RADIUS + 1)]

def row_pass(padded, count):
    taps = tap_list()
    total = taps[0] * padded[0:count]
    for offset in range(1, 2 * RADIUS + 1):
        total = total + taps[offset] * padded[offset:offset + count]
    return total

def col_pass(field):
    taps = tap_list()
    count = field.shape[1]
    padded = jnp.pad(field, ((0, 0), (RADIUS, RADIUS)))
    total = taps[0] * padded[:, 0:count]
    for offset in range(1, 2 * RADIUS + 1):
        total = total + taps[offset] * padded[:, offset:offset + count]
    return total

def edge_sums(start, count, whole):
    positions = start + jnp.arange(count, dtype=jnp.int32)
    total = jnp.zeros((count,), jnp.float32)
    for offset in range(-RADIUS, RADIUS + 1):
        inside = ((positions + offset >= 0) & (positions + offset < whole)).astype(jnp.float32)
        total = total + float(RADIUS + 1 - abs(offset)) * inside
    return total

def project(tilde, passive):
    bottom = jnp.tanh(sharpness * threshold) + jnp.tanh(sharpness * (1.0 - threshold))
    steep = jnp.tanh(sharpness * (tilde - threshold))
    value = (jnp.tanh(sharpness * threshold) + steep) / bottom
    slope = sharpness * (1.0 - steep * steep) / bottom
    solid = passive > 0
    density = jnp.where(solid, 1.0, value)
    slope = jnp.where(solid, 0.0, slope)
    stiffness = exponent * density * density * (1.0 - soft_floor)
    return (stiffness, slope)

def bilinear(table, left, right):
    total = None
    for row_pos in range(4):
        inner = table[row_pos][0] * right[0]
        for col_pos in range(1, 4):
            inner = inner + table[row_pos][col_pos] * right[col_pos]
        term = left[row_pos] * inner
        total = term if total is None else total + term
    return total

def corners(nodes, below):
    stacked = jnp.concatenate([nodes, below], axis=0)
    right_col = jnp.zeros((stacked.shape[0], 1), stacked.dtype)
    shifted = jnp.concatenate([stacked[:, 1:], right_col], axis=1)
    return (stacked[:-1], shifted[:-1], stacked[1:], shifted[1:])

def element_terms(fields, fields_below, duals, duals_below, stiffness, omega):
    state_real = corners(fields[0], fields_below[0])
    state_imag = corners(fields[1], fields_below[1])
    adjoint_real = corners(duals[0], duals_below[0])
    adjoint_imag = corners(duals[1], duals_below[1])
    elastic = bilinear(stiff_table, adjoint_real, state_real) - bilinear(stiff_table, adjoint_imag, state_imag)
    damped = bilinear(stiff_table, adjoint_real, state_imag) + bilinear(stiff_table, adjoint_imag, state_real)
    inertia = bilinear(mass_table, adjoint_real, state_real) - bilinear(mass_table, adjoint_imag, state_imag)
    return stiffness * (elastic - loss_factor * damped) - omega * inertia

def reference(design, passive, state, adjoint, omega_sq, assign):
    weight_sum = edge_sums(0, NR, NR)[:, None] * edge_sums(0, NC, NC)[None, :]
    padded = jnp.pad(design, ((RADIUS, RADIUS), (0, 0)))
    tilde = col_pass(row_pass(padded, NR)) / weight_sum
    stiffness, slope = project(tilde, passive)
    factor = slope / weight_sum
    below = jnp.zeros((2, 1, NC), jnp.float32)

    def step(total, slot):
        fields = lax.dynamic_index_in_dim(state, slot, 1, keepdims=False).astype(jnp.float32)
        duals = lax.dynamic_index_in_dim(adjoint, slot, 1, keepdims=False).astype(jnp.float32)
        omega = omega_sq[assign[slot].astype(jnp.int32)]
        return (total + element_terms(fields, below, duals, below, stiffness, omega), None)
    summed, unused = lax.scan(step, jnp.zeros((NR, NC), jnp.float32), jnp.arange(NF, dtype=jnp.int32))
    spread = summed * factor
    back = col_pass(row_pass(jnp.pad(spread, ((RADIUS, RADIUS), (0, 0))), NR))
    total = jnp.sum(back * back)
    return back * lax.rsqrt(total / (NR * NC) + epsilon)
```

```python
import functools

import jax
import jax.numpy as jnp
from jax import lax
from jax.experimental import pallas as pl
from jax.experimental.pallas import tpu as pltpu
from jax.sharding import PartitionSpec as P

MESH = pl.DeviceIdType.MESH
RADIUS = 8
SHARP = 8.0
EPSILON = 1e-06
CHUNK = 2048
SUB = 512
LAGS = (2, 2, 2, 2)
BIG = 32767.0


def ds(start, size):
    return pl.ds(pl.multiple_of(start, 128), size)


def wide(tile, width):
    return jnp.concatenate([tile] * (width // tile.shape[1]), axis=1)


def row_taps(low, mid, high):
    row = lax.broadcasted_iota(jnp.int32, mid.shape, 0)
    total = 9.0 * mid + (low + high)
    for s in range(1, 8):
        keep = row >= s
        mixed = float(9 - s) * jnp.where(keep, mid, high) + float(1 + s) * jnp.where(keep, low, mid)
        total = total + pltpu.roll(mixed, 8 - s, 0)
    return total


def col_taps(window):
    width = window.shape[1]

    def ahead(x, k):
        return pltpu.roll(x, width - k, 1)

    def behind(x, k):
        return pltpu.roll(x, k, 1)

    for move in (ahead, behind):
        s = window + move(window, 1)
        s = s + move(s, 2)
        s = s + move(s, 4)
        window = s + move(window, 8)
    return window[:, 128 : width - 128]


def edge_gap(distance):
    gap = jnp.maximum(float(RADIUS) - distance, 0.0)
    return 0.5 * gap * (gap + 1.0)


def peak(blocks):
    acc = None
    for block in blocks:
        for t in range(block.shape[1] // 128):
            tile = jnp.abs(block[:, t * 128 : (t + 1) * 128])
            acc = tile if acc is None else jnp.maximum(acc, tile)
    return acc


def to_code(first, second):
    both = jnp.concatenate([first, second], axis=0)
    return jnp.round(both).astype(jnp.int32).astype(jnp.int16)


def from_code(code):
    both = code.astype(jnp.int32).astype(jnp.float32)
    return both[:8], both[8:]


def kernel(sizes, design_h, passive_h, state_h, adjoint_h, omega_sq, assign, back_o, scale_o, *scratch):
    R, F, N, S = sizes
    C = CHUNK
    half, quarter = C // 2, C // 4
    piece = N // F
    n = piece // C
    L1, L3, L4, L5 = LAGS
    (design, passive, state, adjoint, dq, dlo, dhi, nd, nrecv, nbuf, rowed, tmp, own, factor,
     tq, tsc, trecv, tsr, sq, ssc, slo, slos, shi, shis, gq, gsc, grecv, gsr, joined, part, parts,
     in_sem, d_s, d_r, n_s, n_r, t_s, t_r, s_s, s_r, g_s, g_r, p_s, p_r) = scratch
    r = lax.axis_index("rows")
    me = lax.axis_index("freq")
    has_lo = r > 0
    has_hi = r < R - 1
    below_id = {"rows": jnp.maximum(r - 1, 0)}
    above_id = {"rows": jnp.minimum(r + 1, R - 1)}

    loads = [
        pltpu.make_async_copy(design_h, design, in_sem.at[0]),
        pltpu.make_async_copy(passive_h, passive, in_sem.at[1]),
        pltpu.make_async_copy(state_h, state.at[:, :, :, pl.ds(0, N)], in_sem.at[2]),
        pltpu.make_async_copy(adjoint_h, adjoint.at[:, :, :, pl.ds(0, N)], in_sem.at[3]),
    ]
    for load in loads:
        load.start()

    bar = pltpu.get_barrier_semaphore()
    for d in range(1, R):
        pl.semaphore_signal(bar, inc=1, device_id={"rows": lax.rem(r + d, R)}, device_id_type=MESH)
    for d in range(1, F):
        pl.semaphore_signal(bar, inc=1, device_id={"freq": lax.rem(me + d, F)}, device_id_type=MESH)

    edge = jnp.zeros((8, 128), jnp.float32)
    for buf in (rowed, joined):
        buf[:, pl.ds(0, 128)] = edge
        buf[:, pl.ds(N + 128, 128)] = edge
    for buf in (state, adjoint):
        for j in range(2):
            for s in range(S):
                buf[j, s, :, pl.ds(N, 128)] = edge.astype(jnp.bfloat16)
    nbuf[:, pl.ds(N, 128)] = jnp.zeros((nbuf.shape[0], 128), jnp.float32)

    @pl.when(jnp.logical_not(has_lo))
    def _():
        def fill(g, c):
            dlo[g] = jnp.zeros((16, half), jnp.int16)
            return c

        lax.fori_loop(0, F * n, fill, 0)

        def fill2(g, c):
            slo[g] = jnp.zeros((16, half), jnp.int16)
            slos[g] = edge
            return c

        lax.fori_loop(0, n, fill2, 0)

    @pl.when(jnp.logical_not(has_hi))
    def _():
        def fill(g, c):
            dhi[g] = jnp.zeros((16, half), jnp.int16)
            for s in range(S):
                nrecv[g, s] = jnp.zeros((16, quarter), jnp.bfloat16)
            return c

        lax.fori_loop(0, F * n, fill, 0)

        def fill2(g, c):
            shi[g] = jnp.zeros((16, half), jnp.int16)
            shis[g] = edge
            return c

        lax.fori_loop(0, n, fill2, 0)

    lo_on = has_lo.astype(jnp.float32)
    hi_on = has_hi.astype(jnp.float32)
    row = lax.broadcasted_iota(jnp.int32, (8, 128), 0)
    place = (r * 8 + row).astype(jnp.float32)
    row_inv = 1.0 / (81.0 - edge_gap(place) - edge_gap(float(R * 8 - 1) - place))
    omegas = []
    for s in range(S):
        picked = jnp.float32(0.0)
        for t in range(omega_sq.shape[0]):
            picked = picked + jnp.where(assign[s] == t, omega_sq[t], 0.0)
        omegas.append(picked)

    def remote(src, dst, send, recv, device):
        return pltpu.make_async_remote_copy(
            src_ref=src, dst_ref=dst, send_sem=send, recv_sem=recv, device_id=device, device_id_type=MESH
        )

    def d_up(g):
        return remote(dq.at[g], dlo.at[g], d_s.at[0, g], d_r.at[0, g], above_id)

    def d_down(g):
        return remote(dq.at[g], dhi.at[g], d_s.at[1, g], d_r.at[1, g], below_id)

    def n_down(g):
        return remote(nd.at[g], nrecv.at[g], n_s.at[g], n_r.at[g], below_id)

    def t_copies(d, q):
        to = {"freq": lax.rem(me + d, F)}
        return (
            remote(tq.at[d - 1, q], trecv.at[d - 1, q], t_s.at[0, d - 1, q], t_r.at[0, d - 1, q], to),
            remote(tsc.at[d - 1, q], tsr.at[d - 1, q], t_s.at[1, d - 1, q], t_r.at[1, d - 1, q], to),
        )

    def s_up(q):
        return (
            remote(sq.at[q], slo.at[q], s_s.at[0, q], s_r.at[0, q], above_id),
            remote(ssc.at[q], slos.at[q], s_s.at[1, q], s_r.at[1, q], above_id),
        )

    def s_down(q):
        return (
            remote(sq.at[q], shi.at[q], s_s.at[2, q], s_r.at[2, q], below_id),
            remote(ssc.at[q], shis.at[q], s_s.at[3, q], s_r.at[3, q], below_id),
        )

    def g_copies(d, q):
        to = {"freq": lax.rem(me + d, F)}
        return (
            remote(gq.at[q], grecv.at[d - 1, q], g_s.at[0, d - 1, q], g_r.at[0, d - 1, q], to),
            remote(gsc.at[q], gsr.at[d - 1, q], g_s.at[1, d - 1, q], g_r.at[1, d - 1, q], to),
        )

    def encode(load, code_ref, scale_ref):
        acc = None
        for b in range(C // SUB):
            tile = peak([load(b * SUB, SUB)])
            acc = tile if acc is None else jnp.maximum(acc, tile)
        fine = acc > 1e-30
        scale_ref[...] = jnp.where(fine, acc * (1.0 / BIG), 0.0)
        inv = wide(jnp.where(fine, BIG / jnp.where(fine, acc, 1.0), 0.0), SUB)
        for b in range(half // SUB):
            code_ref[:, pl.ds(b * SUB, SUB)] = to_code(
                load(b * SUB, SUB) * inv, load(half + b * SUB, SUB) * inv
            )

    def stage0(k):
        for p in range(F):
            g = p * n + k
            col = g * C
            for b in range(half // SUB):
                x0 = design[:, ds(col + b * SUB, SUB)]
                x1 = design[:, ds(col + half + b * SUB, SUB)]
                dq[g, :, pl.ds(b * SUB, SUB)] = to_code((x0 - 0.5) * 65536.0, (x1 - 0.5) * 65536.0)
            rows16 = lax.broadcasted_iota(jnp.int32, (8, quarter), 0)
            for s in range(S):
                packs = []
                for src in (state, adjoint):
                    acc = jnp.zeros((8, quarter), jnp.float32)
                    for j in range(2):
                        x = src[j, s, :, ds(col, C)].astype(jnp.float32)[0:1]
                        for b in range(4):
                            line = jnp.broadcast_to(x[:, b * quarter : (b + 1) * quarter], (8, quarter))
                            acc = jnp.where(rows16 == j * 4 + b, line, acc)
                    packs.append(acc)
                nd[g, s] = jnp.concatenate(packs, axis=0).astype(jnp.bfloat16)

    def send0(k):
        for p in range(F):
            g = p * n + k

            @pl.when(has_hi)
            def _():
                d_up(g).start()

            @pl.when(has_lo)
            def _():
                d_down(g).start()
                n_down(g).start()

    def stage1(k):
        for p in range(F):
            g = p * n + k
            col = g * C

            @pl.when(has_lo)
            def _():
                d_up(g).wait_recv()

            @pl.when(has_hi)
            def _():
                d_down(g).wait_recv()
                n_down(g).wait_recv()

            for s in range(S):
                rows16 = nrecv[g, s].astype(jnp.float32)
                for t in range(4):
                    for b in range(4):
                        nbuf[pl.ds(s * 8 + t, 1), ds(col + b * quarter, quarter)] = rows16[
                            t * 4 + b : t * 4 + b + 1
                        ]
            for b in range(half // SUB):
                lows = from_code(dlo[g, :, pl.ds(b * SUB, SUB)])
                highs = from_code(dhi[g, :, pl.ds(b * SUB, SUB)])
                for h in range(2):
                    at = col + h * half + b * SUB
                    low = (lows[h] * (1.0 / 65536.0) + 0.5) * lo_on
                    high = (highs[h] * (1.0 / 65536.0) + 0.5) * hi_on
                    rowed[:, ds(at + 128, SUB)] = row_taps(low, design[:, ds(at, SUB)], high)

    row_sub = lax.broadcasted_iota(jnp.int32, (8, SUB + 128), 0)

    def haar(src, j, s, t, at):
        x = src[j, s, :, ds(at, SUB + 128)].astype(jnp.float32)
        next_line = nbuf[pl.ds(s * 8 + t, 1), ds(at, SUB + 128)]
        below = jnp.where(row_sub == 7, next_line, pltpu.roll(x, 7, 0))
        out = []
        for y in (x + below, x - below):
            right = pltpu.roll(y, SUB + 127, 1)[:, :SUB]
            y = y[:, :SUB]
            out.extend((y + right, y - right))
        return out

    def terms(at):
        j = (at + lax.broadcasted_iota(jnp.int32, (1, SUB), 1)).astype(jnp.float32)
        col_inv = 1.0 / (81.0 - edge_gap(j) - edge_gap(float(N - 1) - j))
        weight = wide(row_inv, SUB) * col_inv
        tilde = col_taps(rowed[:, ds(at, SUB + 256)]) * weight
        top = jnp.tanh(jnp.full((8, SUB), SHARP * 0.5, jnp.float32))
        inv_q = 0.5 / top
        t = jnp.tanh(SHARP * (tilde - 0.5))
        solid = passive[:, ds(at, SUB)] > 0
        density = jnp.where(solid, 1.0, (top + t) * inv_q)
        slope = jnp.where(solid, 0.0, SHARP * (1.0 - t * t) * inv_q)
        stiff = 3.0 * density * density * (1.0 - 0.001)
        total = None
        for s in range(S):
            sr = haar(state, 0, s, 0, at)
            si = haar(state, 1, s, 1, at)
            ar = haar(adjoint, 0, s, 2, at)
            ai = haar(adjoint, 1, s, 3, at)
            direct = [ar[c] * sr[c] - ai[c] * si[c] for c in range(4)]
            cross = [ar[c] * si[c] + ai[c] * sr[c] for c in range(1, 4)]
            mix = [None] + [direct[c] - 0.2 * cross[c - 1] for c in range(1, 4)]
            stiffly = 0.25 * (mix[1] + mix[2]) + (1.0 / 6.0) * mix[3]
            mass = (1.0 / 16.0) * direct[0] + (1.0 / 48.0) * (direct[1] + direct[2]) + (1.0 / 144.0) * direct[3]
            value = stiff * stiffly - omegas[s] * mass
            total = value if total is None else total + value
        return total, slope * weight

    def stage2(q):
        for d in range(1, F):
            col = (lax.rem(me + d, F) * n + q) * C

            def body(b, c):
                value, unused = terms(col + b * SUB)
                tmp[:, ds(b * SUB, SUB)] = value
                return c

            lax.fori_loop(0, C // SUB, body, 0)
            encode(lambda o, w: tmp[:, pl.ds(o, w)], tq.at[d - 1, q], tsc.at[d - 1, q])
        col = (me * n + q) * C

        def body(b, c):
            value, slope = terms(col + b * SUB)
            own[:, ds(q * C + b * SUB, SUB)] = value
            factor[:, ds(q * C + b * SUB, SUB)] = slope
            return c

        lax.fori_loop(0, C // SUB, body, 0)
        for d in range(1, F):
            for copy in t_copies(d, q):
                copy.start()

    def stage3(q):
        for d in range(1, F):
            for copy in t_copies(d, q):
                copy.wait_recv()
        for b in range(half // SUB):
            sums = [own[:, ds(q * C + h * half + b * SUB, SUB)] for h in range(2)]
            for d in range(1, F):
                got = from_code(trecv[d - 1, q, :, pl.ds(b * SUB, SUB)])
                scale = wide(tsr[d - 1, q], SUB)
                sums = [sums[h] + got[h] * scale for h in range(2)]
            for h in range(2):
                at = q * C + h * half + b * SUB
                own[:, ds(at, SUB)] = sums[h] * factor[:, ds(at, SUB)]
        encode(lambda o, w: own[:, ds(q * C + o, w)], sq.at[q], ssc.at[q])

    def send3(q):
        @pl.when(has_hi)
        def _():
            for copy in s_up(q):
                copy.start()

        @pl.when(has_lo)
        def _():
            for copy in s_down(q):
                copy.start()

    def stage4(q):
        @pl.when(has_lo)
        def _():
            for copy in s_up(q):
                copy.wait_recv()

        @pl.when(has_hi)
        def _():
            for copy in s_down(q):
                copy.wait_recv()

        base = (me * n + q) * C + 128
        for b in range(half // SUB):
            lows = from_code(slo[q, :, pl.ds(b * SUB, SUB)])
            highs = from_code(shi[q, :, pl.ds(b * SUB, SUB)])
            los, his = wide(slos[q], SUB), wide(shis[q], SUB)
            for h in range(2):
                at = h * half + b * SUB
                joined[:, ds(base + at, SUB)] = row_taps(
                    lows[h] * los, own[:, ds(q * C + at, SUB)], highs[h] * his
                )
        encode(lambda o, w: joined[:, ds(base + o, w)], gq.at[q], gsc.at[q])

    def send4(q):
        for d in range(1, F):
            for copy in g_copies(d, q):
                copy.start()

    def stage5(q):
        for d in range(1, F):
            for copy in g_copies(d, q):
                copy.wait_recv()
            base = (lax.rem(me + F - d, F) * n + q) * C + 128
            scale = wide(gsr[d - 1, q], SUB)
            for b in range(half // SUB):
                got = from_code(grecv[d - 1, q, :, pl.ds(b * SUB, SUB)])
                for h in range(2):
                    joined[:, ds(base + h * half + b * SUB, SUB)] = got[h] * scale

    for load in loads:
        load.wait()
    pl.semaphore_wait(bar, R - 1 + F - 1)

    o1 = L1
    o2 = o1 + 2
    o3 = o2 + L3
    o4 = o3 + L4
    o5 = o4 + L5

    def guarded(fn, it, offset, turn):
        i = it - offset
        arg = lax.rem(i + 1 + n, n) if turn else i

        @pl.when((i >= 0) & (i < n))
        def _():
            fn(arg)

    def step(it, carry):
        guarded(stage0, it, 0, False)
        guarded(stage3, it, o3, True)
        guarded(send0, it, 0, False)
        guarded(stage4, it, o4, True)
        guarded(send3, it, o3, True)
        guarded(stage1, it, o1, False)
        guarded(send4, it, o4, True)
        guarded(stage2, it, o2, True)
        guarded(stage5, it, o5, True)
        return carry

    lax.fori_loop(0, n + o5, step, 0)

    def last(b, acc):
        at = b * SUB
        value = col_taps(joined[:, ds(at, SUB + 256)])
        back_o[:, ds(at, SUB)] = value
        for t in range(SUB // 128):
            tile = value[:, t * 128 : (t + 1) * 128]
            acc = acc + tile * tile
        return acc

    part[...] = lax.fori_loop(0, N // SUB, last, edge)

    def send_waits(k, c):
        for p in range(F):
            g = p * n + k

            @pl.when(has_hi)
            def _():
                d_up(g).wait_send()

            @pl.when(has_lo)
            def _():
                d_down(g).wait_send()
                n_down(g).wait_send()

        for d in range(1, F):
            for copy in t_copies(d, k) + g_copies(d, k):
                copy.wait_send()

        @pl.when(has_hi)
        def _():
            for copy in s_up(k):
                copy.wait_send()

        @pl.when(has_lo)
        def _():
            for copy in s_down(k):
                copy.wait_send()

        return c

    lax.fori_loop(0, n, send_waits, 0)

    def sum_copy(d):
        return remote(part, parts.at[d - 1], p_s.at[d - 1], p_r.at[d - 1], {"rows": lax.rem(r + d, R)})

    for d in range(1, R):
        sum_copy(d).start()
    acc = part[...]
    for d in range(1, R):
        sum_copy(d).wait_recv()
        acc = acc + parts[d - 1]
    total = jnp.sum(acc, keepdims=True)
    scale_o[...] = jnp.broadcast_to(lax.rsqrt(total / float(R * 8 * N) + EPSILON), (8, 128))
    for d in range(1, R):
        sum_copy(d).wait_send()


def shards(sizes, design, passive, state, adjoint, omega_sq, assign):
    R, F, N, S = sizes
    C = CHUNK
    half, quarter = C // 2, C // 4
    piece = N // F
    n = piece // C
    G = F * n
    f32, i16, bf16 = jnp.float32, jnp.int16, jnp.bfloat16
    V = pltpu.VMEM
    dma = pltpu.SemaphoreType.DMA
    scratch = [
        V((8, N), f32), V((8, N), jnp.int32), V((2, S, 8, N + 128), bf16), V((2, S, 8, N + 128), bf16),
        V((G, 16, half), i16), V((G, 16, half), i16), V((G, 16, half), i16),
        V((G, S, 16, quarter), bf16), V((G, S, 16, quarter), bf16), V((8 * S, N + 128), f32),
        V((8, N + 256), f32), V((8, C), f32), V((8, piece), f32), V((8, piece), f32),
        V((F - 1, n, 16, half), i16), V((F - 1, n, 8, 128), f32),
        V((F - 1, n, 16, half), i16), V((F - 1, n, 8, 128), f32),
        V((n, 16, half), i16), V((n, 8, 128), f32),
        V((n, 16, half), i16), V((n, 8, 128), f32), V((n, 16, half), i16), V((n, 8, 128), f32),
        V((n, 16, half), i16), V((n, 8, 128), f32),
        V((F - 1, n, 16, half), i16), V((F - 1, n, 8, 128), f32),
        V((8, N + 256), f32), V((8, 128), f32), V((R - 1, 8, 128), f32),
        dma((4,)), dma((2, G)), dma((2, G)), dma((G,)), dma((G,)),
        dma((2, F - 1, n)), dma((2, F - 1, n)), dma((4, n)), dma((4, n)),
        dma((2, F - 1, n)), dma((2, F - 1, n)), dma((R - 1,)), dma((R - 1,)),
    ]
    anywhere = pl.BlockSpec(memory_space=pl.ANY)
    small = pl.BlockSpec(memory_space=pltpu.SMEM)
    vmem = pl.BlockSpec(memory_space=pltpu.VMEM)
    back, scale = pl.pallas_call(
        functools.partial(kernel, sizes),
        out_shape=(jax.ShapeDtypeStruct((8, N), f32), jax.ShapeDtypeStruct((8, 128), f32)),
        in_specs=[anywhere] * 4 + [small] * 2,
        out_specs=(vmem, vmem),
        scratch_shapes=scratch,
        compiler_params=pltpu.CompilerParams(
            collective_id=0, has_side_effects=True, vmem_limit_bytes=60 * 1024 * 1024
        ),
    )(design, passive, state, adjoint, omega_sq, assign)
    return back * scale[:1, :1]


def solution(mesh):
    R, F = mesh.shape["rows"], mesh.shape["freq"]

    def run(design, passive, state, adjoint, omega_sq, assign):
        sizes = (R, F, design.shape[1], state.shape[1])
        return shards(sizes, design, passive, state, adjoint, omega_sq, assign)

    return jax.shard_map(
        run,
        mesh=mesh,
        in_specs=(
            P("rows", None),
            P("rows", None),
            P(None, "freq", "rows", None),
            P(None, "freq", "rows", None),
            P(),
            P("freq"),
        ),
        out_specs=P("rows", None),
        check_vma=False,
    )
```

```python
import functools

import jax
import jax.numpy as jnp
from jax import lax
from jax.experimental import pallas as pl
from jax.experimental.pallas import tpu as pltpu
from jax.sharding import PartitionSpec as P

MESH = pl.DeviceIdType.MESH
RADIUS = 8
SHARP = 8.0
EPSILON = 1e-06
CHUNK = 2048
SUB = 512
CSUB = 1024
TSUB = 512
TUN = 4
CUN = 2
LUN = 4
LAGS = (2, 2, 2, 2)
BIG = 32767.0


def ds(start, size):
    return pl.ds(pl.multiple_of(start, 128), size)


def wide(tile, width):
    return jnp.concatenate([tile] * (width // tile.shape[1]), axis=1)


def row_taps(low, mid, high):
    row = lax.broadcasted_iota(jnp.int32, mid.shape, 0)
    total = 9.0 * mid + (low + high)
    for s in range(1, 8):
        keep = row >= s
        mixed = float(9 - s) * jnp.where(keep, mid, high) + float(1 + s) * jnp.where(keep, low, mid)
        total = total + pltpu.roll(mixed, 8 - s, 0)
    return total


def col_taps(window):
    width = window.shape[1]

    def ahead(x, k):
        return pltpu.roll(x, width - k, 1)

    def behind(x, k):
        return pltpu.roll(x, k, 1)

    for move in (ahead, behind):
        s = window + move(window, 1)
        s = s + move(s, 2)
        s = s + move(s, 4)
        window = s + move(window, 8)
    return window[:, 128 : width - 128]


def edge_gap(distance):
    gap = jnp.maximum(float(RADIUS) - distance, 0.0)
    return 0.5 * gap * (gap + 1.0)


def peak(blocks):
    acc = None
    for block in blocks:
        for t in range(block.shape[1] // 128):
            tile = jnp.abs(block[:, t * 128 : (t + 1) * 128])
            acc = tile if acc is None else jnp.maximum(acc, tile)
    return acc


def to_code(first, second):
    both = jnp.concatenate([first, second], axis=0)
    return jnp.round(both).astype(jnp.int32).astype(jnp.int16)


def from_code(code):
    both = code.astype(jnp.int32).astype(jnp.float32)
    return both[:8], both[8:]


def kernel(sizes, design_h, passive_h, state_h, adjoint_h, omega_sq, assign, back_o, scale_o, *scratch):
    R, F, N, S = sizes
    C = CHUNK
    half, quarter = C // 2, C // 4
    piece = N // F
    n = piece // C
    L1, L3, L4, L5 = LAGS
    (design, passive, state, adjoint, dq, dlo, dhi, nd, nrecv, nbuf, rowed, tmp, filt, own, factor,
     tq, tsc, trecv, tsr, sq, ssc, slo, slos, shi, shis, gq, gsc, grecv, gsr, joined, part, parts,
     in_sem, d_s, d_r, n_s, n_r, t_s, t_r, s_s, s_r, g_s, g_r, p_s, p_r) = scratch
    r = lax.axis_index("rows")
    me = lax.axis_index("freq")
    has_lo = r > 0
    has_hi = r < R - 1
    below_id = {"rows": jnp.maximum(r - 1, 0)}
    above_id = {"rows": jnp.minimum(r + 1, R - 1)}

    loads = [
        pltpu.make_async_copy(design_h, design, in_sem.at[0]),
        pltpu.make_async_copy(passive_h, passive, in_sem.at[1]),
        pltpu.make_async_copy(state_h, state.at[:, :, :, pl.ds(0, N)], in_sem.at[2]),
        pltpu.make_async_copy(adjoint_h, adjoint.at[:, :, :, pl.ds(0, N)], in_sem.at[3]),
    ]
    for load in loads:
        load.start()

    bar = pltpu.get_barrier_semaphore()
    for d in range(1, R):
        pl.semaphore_signal(bar, inc=1, device_id={"rows": lax.rem(r + d, R)}, device_id_type=MESH)
    for d in range(1, F):
        pl.semaphore_signal(bar, inc=1, device_id={"freq": lax.rem(me + d, F)}, device_id_type=MESH)

    edge = jnp.zeros((8, 128), jnp.float32)
    for buf in (rowed, joined):
        buf[:, pl.ds(0, 128)] = edge
        buf[:, pl.ds(N + 128, 128)] = edge
    for buf in (state, adjoint):
        for j in range(2):
            for s in range(S):
                buf[j, s, :, pl.ds(N, 128)] = edge.astype(jnp.bfloat16)
    nbuf[:, pl.ds(N, 128)] = jnp.zeros((nbuf.shape[0], 128), jnp.float32)

    @pl.when(jnp.logical_not(has_lo))
    def _():
        def fill(g, c):
            dlo[g] = jnp.zeros((16, half), jnp.int16)
            return c

        lax.fori_loop(0, F * n, fill, 0)

        def fill2(g, c):
            slo[g] = jnp.zeros((16, half), jnp.int16)
            slos[g] = edge
            return c

        lax.fori_loop(0, n, fill2, 0)

    @pl.when(jnp.logical_not(has_hi))
    def _():
        def fill(g, c):
            dhi[g] = jnp.zeros((16, half), jnp.int16)
            for s in range(S):
                nrecv[g, s] = jnp.zeros((16, quarter), jnp.bfloat16)
            return c

        lax.fori_loop(0, F * n, fill, 0)

        def fill2(g, c):
            shi[g] = jnp.zeros((16, half), jnp.int16)
            shis[g] = edge
            return c

        lax.fori_loop(0, n, fill2, 0)

    lo_on = has_lo.astype(jnp.float32)
    hi_on = has_hi.astype(jnp.float32)
    row = lax.broadcasted_iota(jnp.int32, (8, 128), 0)
    place = (r * 8 + row).astype(jnp.float32)
    row_inv = 1.0 / (81.0 - edge_gap(place) - edge_gap(float(R * 8 - 1) - place))
    omegas = []
    for s in range(S):
        picked = jnp.float32(0.0)
        for t in range(omega_sq.shape[0]):
            picked = picked + jnp.where(assign[s] == t, omega_sq[t], 0.0)
        omegas.append(picked)

    def remote(src, dst, send, recv, device):
        return pltpu.make_async_remote_copy(
            src_ref=src, dst_ref=dst, send_sem=send, recv_sem=recv, device_id=device, device_id_type=MESH
        )

    def d_up(g):
        return remote(dq.at[g], dlo.at[g], d_s.at[0, g], d_r.at[0, g], above_id)

    def d_down(g):
        return remote(dq.at[g], dhi.at[g], d_s.at[1, g], d_r.at[1, g], below_id)

    def n_down(g):
        return remote(nd.at[g], nrecv.at[g], n_s.at[g], n_r.at[g], below_id)

    def t_copies(d, q):
        to = {"freq": lax.rem(me + d, F)}
        return (
            remote(tq.at[d - 1, q], trecv.at[d - 1, q], t_s.at[0, d - 1, q], t_r.at[0, d - 1, q], to),
            remote(tsc.at[d - 1, q], tsr.at[d - 1, q], t_s.at[1, d - 1, q], t_r.at[1, d - 1, q], to),
        )

    def s_up(q):
        return (
            remote(sq.at[q], slo.at[q], s_s.at[0, q], s_r.at[0, q], above_id),
            remote(ssc.at[q], slos.at[q], s_s.at[1, q], s_r.at[1, q], above_id),
        )

    def s_down(q):
        return (
            remote(sq.at[q], shi.at[q], s_s.at[2, q], s_r.at[2, q], below_id),
            remote(ssc.at[q], shis.at[q], s_s.at[3, q], s_r.at[3, q], below_id),
        )

    def g_copies(d, q):
        to = {"freq": lax.rem(me + d, F)}
        return (
            remote(gq.at[q], grecv.at[d - 1, q], g_s.at[0, d - 1, q], g_r.at[0, d - 1, q], to),
            remote(gsc.at[q], gsr.at[d - 1, q], g_s.at[1, d - 1, q], g_r.at[1, d - 1, q], to),
        )

    def encode(load, code_ref, scale_ref):
        acc = None
        for b in range(C // SUB):
            tile = peak([load(b * SUB, SUB)])
            acc = tile if acc is None else jnp.maximum(acc, tile)
        fine = acc > 1e-30
        scale_ref[...] = jnp.where(fine, acc * (1.0 / BIG), 0.0)
        inv = wide(jnp.where(fine, BIG / jnp.where(fine, acc, 1.0), 0.0), SUB)
        for b in range(half // SUB):
            code_ref[:, pl.ds(b * SUB, SUB)] = to_code(
                load(b * SUB, SUB) * inv, load(half + b * SUB, SUB) * inv
            )

    def stage0(k):
        for p in range(F):
            g = p * n + k
            col = g * C
            for b in range(half // SUB):
                x0 = design[:, ds(col + b * SUB, SUB)]
                x1 = design[:, ds(col + half + b * SUB, SUB)]
                dq[g, :, pl.ds(b * SUB, SUB)] = to_code((x0 - 0.5) * 65536.0, (x1 - 0.5) * 65536.0)
            rows16 = lax.broadcasted_iota(jnp.int32, (8, quarter), 0)
            for s in range(S):
                packs = []
                for src in (state, adjoint):
                    acc = jnp.zeros((8, quarter), jnp.float32)
                    for j in range(2):
                        x = src[j, s, :, ds(col, C)].astype(jnp.float32)[0:1]
                        for b in range(4):
                            line = jnp.broadcast_to(x[:, b * quarter : (b + 1) * quarter], (8, quarter))
                            acc = jnp.where(rows16 == j * 4 + b, line, acc)
                    packs.append(acc)
                nd[g, s] = jnp.concatenate(packs, axis=0).astype(jnp.bfloat16)

    def send0(k):
        for p in range(F):
            g = p * n + k

            @pl.when(has_hi)
            def _():
                d_up(g).start()

            @pl.when(has_lo)
            def _():
                d_down(g).start()
                n_down(g).start()

    def stage1(k):
        for p in range(F):
            g = p * n + k
            col = g * C

            @pl.when(has_lo)
            def _():
                d_up(g).wait_recv()

            @pl.when(has_hi)
            def _():
                d_down(g).wait_recv()
                n_down(g).wait_recv()

            for s in range(S):
                rows16 = nrecv[g, s].astype(jnp.float32)
                for t in range(4):
                    for b in range(4):
                        nbuf[pl.ds(s * 8 + t, 1), ds(col + b * quarter, quarter)] = rows16[
                            t * 4 + b : t * 4 + b + 1
                        ]
            for b in range(half // SUB):
                lows = from_code(dlo[g, :, pl.ds(b * SUB, SUB)])
                highs = from_code(dhi[g, :, pl.ds(b * SUB, SUB)])
                for h in range(2):
                    at = col + h * half + b * SUB
                    low = (lows[h] * (1.0 / 65536.0) + 0.5) * lo_on
                    high = (highs[h] * (1.0 / 65536.0) + 0.5) * hi_on
                    rowed[:, ds(at + 128, SUB)] = row_taps(low, design[:, ds(at, SUB)], high)

    row_sub = lax.broadcasted_iota(jnp.int32, (8, TSUB + 128), 0)

    def haar(src, j, s, t, at):
        x = src[j, s, :, ds(at, TSUB + 128)].astype(jnp.float32)
        next_line = nbuf[pl.ds(s * 8 + t, 1), ds(at, TSUB + 128)]
        below = jnp.where(row_sub == 7, next_line, pltpu.roll(x, 7, 0))
        out = []
        for y in (x + below, x - below):
            right = pltpu.roll(y, TSUB + 127, 1)[:, :TSUB]
            y = y[:, :TSUB]
            out.extend((y + right, y - right))
        return out

    def terms(at, o):
        j = (at + lax.broadcasted_iota(jnp.int32, (1, TSUB), 1)).astype(jnp.float32)
        col_inv = 1.0 / (81.0 - edge_gap(j) - edge_gap(float(N - 1) - j))
        weight = wide(row_inv, TSUB) * col_inv
        tilde = filt[:, ds(o, TSUB)] * weight
        top = jnp.tanh(jnp.full((8, TSUB), SHARP * 0.5, jnp.float32))
        inv_q = 0.5 / top
        t = jnp.tanh(SHARP * (tilde - 0.5))
        solid = passive[:, ds(at, TSUB)] > 0
        density = jnp.where(solid, 1.0, (top + t) * inv_q)
        slope = jnp.where(solid, 0.0, SHARP * (1.0 - t * t) * inv_q)
        stiff = 3.0 * density * density * (1.0 - 0.001)
        total = None
        for s in range(S):
            sr = haar(state, 0, s, 0, at)
            si = haar(state, 1, s, 1, at)
            ar = haar(adjoint, 0, s, 2, at)
            ai = haar(adjoint, 1, s, 3, at)
            direct = [ar[c] * sr[c] - ai[c] * si[c] for c in range(4)]
            cross = [ar[c] * si[c] + ai[c] * sr[c] for c in range(1, 4)]
            mix = [None] + [direct[c] - 0.2 * cross[c - 1] for c in range(1, 4)]
            stiffly = 0.25 * (mix[1] + mix[2]) + (1.0 / 6.0) * mix[3]
            mass = (1.0 / 16.0) * direct[0] + (1.0 / 48.0) * (direct[1] + direct[2]) + (1.0 / 144.0) * direct[3]
            value = stiff * stiffly - omegas[s] * mass
            total = value if total is None else total + value
        return total, slope * weight

    def filtered(col):
        def body(b, c):
            filt[:, ds(b * CSUB, CSUB)] = col_taps(rowed[:, ds(col + b * CSUB, CSUB + 256)])
            return c

        lax.fori_loop(0, C // CSUB, body, 0, unroll=CUN)

    def stage2(q):
        for d in range(1, F):
            col = (lax.rem(me + d, F) * n + q) * C

            filtered(col)

            def body(b, c):
                value, unused = terms(col + b * TSUB, b * TSUB)
                tmp[:, ds(b * TSUB, TSUB)] = value
                return c

            lax.fori_loop(0, C // TSUB, body, 0, unroll=TUN)
            encode(lambda o, w: tmp[:, pl.ds(o, w)], tq.at[d - 1, q], tsc.at[d - 1, q])
        col = (me * n + q) * C

        filtered(col)

        def body(b, c):
            value, slope = terms(col + b * TSUB, b * TSUB)
            own[:, ds(q * C + b * TSUB, TSUB)] = value
            factor[:, ds(q * C + b * TSUB, TSUB)] = slope
            return c

        lax.fori_loop(0, C // TSUB, body, 0, unroll=TUN)
        for d in range(1, F):
            for copy in t_copies(d, q):
                copy.start()

    def stage3(q):
        for d in range(1, F):
            for copy in t_copies(d, q):
                copy.wait_recv()
        for b in range(half // SUB):
            sums = [own[:, ds(q * C + h * half + b * SUB, SUB)] for h in range(2)]
            for d in range(1, F):
                got = from_code(trecv[d - 1, q, :, pl.ds(b * SUB, SUB)])
                scale = wide(tsr[d - 1, q], SUB)
                sums = [sums[h] + got[h] * scale for h in range(2)]
            for h in range(2):
                at = q * C + h * half + b * SUB
                own[:, ds(at, SUB)] = sums[h] * factor[:, ds(at, SUB)]
        encode(lambda o, w: own[:, ds(q * C + o, w)], sq.at[q], ssc.at[q])

    def send3(q):
        @pl.when(has_hi)
        def _():
            for copy in s_up(q):
                copy.start()

        @pl.when(has_lo)
        def _():
            for copy in s_down(q):
                copy.start()

    def stage4(q):
        @pl.when(has_lo)
        def _():
            for copy in s_up(q):
                copy.wait_recv()

        @pl.when(has_hi)
        def _():
            for copy in s_down(q):
                copy.wait_recv()

        base = (me * n + q) * C + 128
        for b in range(half // SUB):
            lows = from_code(slo[q, :, pl.ds(b * SUB, SUB)])
            highs = from_code(shi[q, :, pl.ds(b * SUB, SUB)])
            los, his = wide(slos[q], SUB), wide(shis[q], SUB)
            for h in range(2):
                at = h * half + b * SUB
                joined[:, ds(base + at, SUB)] = row_taps(
                    lows[h] * los, own[:, ds(q * C + at, SUB)], highs[h] * his
                )
        encode(lambda o, w: joined[:, ds(base + o, w)], gq.at[q], gsc.at[q])

    def send4(q):
        for d in range(1, F):
            for copy in g_copies(d, q):
                copy.start()

    def stage5(q):
        for d in range(1, F):
            for copy in g_copies(d, q):
                copy.wait_recv()
            base = (lax.rem(me + F - d, F) * n + q) * C + 128
            scale = wide(gsr[d - 1, q], SUB)
            for b in range(half // SUB):
                got = from_code(grecv[d - 1, q, :, pl.ds(b * SUB, SUB)])
                for h in range(2):
                    joined[:, ds(base + h * half + b * SUB, SUB)] = got[h] * scale

    for load in loads:
        load.wait()
    pl.semaphore_wait(bar, R - 1 + F - 1)

    o1 = L1
    o2 = o1 + 2
    o3 = o2 + L3
    o4 = o3 + L4
    o5 = o4 + L5

    def guarded(fn, it, offset, turn):
        i = it - offset
        arg = lax.rem(i + 1 + n, n) if turn else i

        @pl.when((i >= 0) & (i < n))
        def _():
            fn(arg)

    def step(it, carry):
        guarded(stage0, it, 0, False)
        guarded(stage3, it, o3, True)
        guarded(send0, it, 0, False)
        guarded(stage4, it, o4, True)
        guarded(send3, it, o3, True)
        guarded(stage1, it, o1, False)
        guarded(send4, it, o4, True)
        guarded(stage2, it, o2, True)
        guarded(stage5, it, o5, True)
        return carry

    lax.fori_loop(0, n + o5, step, 0)

    def last(b, acc):
        at = b * CSUB
        value = col_taps(joined[:, ds(at, CSUB + 256)])
        back_o[:, ds(at, CSUB)] = value
        for t in range(CSUB // 128):
            tile = value[:, t * 128 : (t + 1) * 128]
            acc = acc + tile * tile
        return acc

    part[...] = lax.fori_loop(0, N // CSUB, last, edge, unroll=LUN)

    def send_waits(k, c):
        for p in range(F):
            g = p * n + k

            @pl.when(has_hi)
            def _():
                d_up(g).wait_send()

            @pl.when(has_lo)
            def _():
                d_down(g).wait_send()
                n_down(g).wait_send()

        for d in range(1, F):
            for copy in t_copies(d, k) + g_copies(d, k):
                copy.wait_send()

        @pl.when(has_hi)
        def _():
            for copy in s_up(k):
                copy.wait_send()

        @pl.when(has_lo)
        def _():
            for copy in s_down(k):
                copy.wait_send()

        return c

    lax.fori_loop(0, n, send_waits, 0)

    def sum_copy(d):
        return remote(part, parts.at[d - 1], p_s.at[d - 1], p_r.at[d - 1], {"rows": lax.rem(r + d, R)})

    for d in range(1, R):
        sum_copy(d).start()
    acc = part[...]
    for d in range(1, R):
        sum_copy(d).wait_recv()
        acc = acc + parts[d - 1]
    total = jnp.sum(acc, keepdims=True)
    scale_o[...] = jnp.broadcast_to(lax.rsqrt(total / float(R * 8 * N) + EPSILON), (8, 128))
    for d in range(1, R):
        sum_copy(d).wait_send()


def shards(sizes, design, passive, state, adjoint, omega_sq, assign):
    R, F, N, S = sizes
    C = CHUNK
    half, quarter = C // 2, C // 4
    piece = N // F
    n = piece // C
    G = F * n
    f32, i16, bf16 = jnp.float32, jnp.int16, jnp.bfloat16
    V = pltpu.VMEM
    dma = pltpu.SemaphoreType.DMA
    scratch = [
        V((8, N), f32), V((8, N), jnp.int32), V((2, S, 8, N + 128), bf16), V((2, S, 8, N + 128), bf16),
        V((G, 16, half), i16), V((G, 16, half), i16), V((G, 16, half), i16),
        V((G, S, 16, quarter), bf16), V((G, S, 16, quarter), bf16), V((8 * S, N + 128), f32),
        V((8, N + 256), f32), V((8, C), f32), V((8, C), f32), V((8, piece), f32), V((8, piece), f32),
        V((F - 1, n, 16, half), i16), V((F - 1, n, 8, 128), f32),
        V((F - 1, n, 16, half), i16), V((F - 1, n, 8, 128), f32),
        V((n, 16, half), i16), V((n, 8, 128), f32),
        V((n, 16, half), i16), V((n, 8, 128), f32), V((n, 16, half), i16), V((n, 8, 128), f32),
        V((n, 16, half), i16), V((n, 8, 128), f32),
        V((F - 1, n, 16, half), i16), V((F - 1, n, 8, 128), f32),
        V((8, N + 256), f32), V((8, 128), f32), V((R - 1, 8, 128), f32),
        dma((4,)), dma((2, G)), dma((2, G)), dma((G,)), dma((G,)),
        dma((2, F - 1, n)), dma((2, F - 1, n)), dma((4, n)), dma((4, n)),
        dma((2, F - 1, n)), dma((2, F - 1, n)), dma((R - 1,)), dma((R - 1,)),
    ]
    anywhere = pl.BlockSpec(memory_space=pl.ANY)
    small = pl.BlockSpec(memory_space=pltpu.SMEM)
    vmem = pl.BlockSpec(memory_space=pltpu.VMEM)
    back, scale = pl.pallas_call(
        functools.partial(kernel, sizes),
        out_shape=(jax.ShapeDtypeStruct((8, N), f32), jax.ShapeDtypeStruct((8, 128), f32)),
        in_specs=[anywhere] * 4 + [small] * 2,
        out_specs=(vmem, vmem),
        scratch_shapes=scratch,
        compiler_params=pltpu.CompilerParams(
            collective_id=0, has_side_effects=True, vmem_limit_bytes=60 * 1024 * 1024
        ),
    )(design, passive, state, adjoint, omega_sq, assign)
    return back * scale[:1, :1]


def solution(mesh):
    R, F = mesh.shape["rows"], mesh.shape["freq"]

    def run(design, passive, state, adjoint, omega_sq, assign):
        sizes = (R, F, design.shape[1], state.shape[1])
        return shards(sizes, design, passive, state, adjoint, omega_sq, assign)

    return jax.shard_map(
        run,
        mesh=mesh,
        in_specs=(
            P("rows", None),
            P("rows", None),
            P(None, "freq", "rows", None),
            P(None, "freq", "rows", None),
            P(),
            P("freq"),
        ),
        out_specs=P("rows", None),
        check_vma=False,
    )
```

```python
import functools

import jax
import jax.numpy as jnp
from jax import lax
from jax.experimental import pallas as pl
from jax.experimental.pallas import tpu as pltpu
from jax.sharding import PartitionSpec as P

MESH = pl.DeviceIdType.MESH
RADIUS = 8
SHARP = 8.0
EPSILON = 1e-06
CHUNK = 2048
SUB = 512
CSUB = 2048
TSUB = 512
TUN = 4
CUN = 1
LAGS = (2, 3, 2, 2)
BIG = 32767.0


def ds(start, size):
    return pl.ds(pl.multiple_of(start, 128), size)


def wide(tile, width):
    return jnp.concatenate([tile] * (width // tile.shape[1]), axis=1)


def row_taps(low, mid, high):
    row = lax.broadcasted_iota(jnp.int32, mid.shape, 0)
    total = 9.0 * mid + (low + high)
    for s in range(1, 8):
        keep = row >= s
        mixed = float(9 - s) * jnp.where(keep, mid, high) + float(1 + s) * jnp.where(keep, low, mid)
        total = total + pltpu.roll(mixed, 8 - s, 0)
    return total


def col_taps(window):
    width = window.shape[1]

    def ahead(x, k):
        return pltpu.roll(x, width - k, 1)

    def behind(x, k):
        return pltpu.roll(x, k, 1)

    for move in (ahead, behind):
        s = window + move(window, 1)
        s = s + move(s, 2)
        s = s + move(s, 4)
        window = s + move(window, 8)
    return window[:, 128 : width - 128]


def edge_gap(distance):
    gap = jnp.maximum(float(RADIUS) - distance, 0.0)
    return 0.5 * gap * (gap + 1.0)


def peak(blocks):
    acc = None
    for block in blocks:
        for t in range(block.shape[1] // 128):
            tile = jnp.abs(block[:, t * 128 : (t + 1) * 128])
            acc = tile if acc is None else jnp.maximum(acc, tile)
    return acc


def to_code(first, second):
    both = jnp.concatenate([first, second], axis=0)
    return jnp.round(both).astype(jnp.int32).astype(jnp.int16)


def from_code(code):
    both = code.astype(jnp.int32).astype(jnp.float32)
    return both[:8], both[8:]


def kernel(sizes, design_h, passive_h, state_h, adjoint_h, omega_sq, assign, back_o, scale_o, *scratch):
    R, F, N, S = sizes
    C = CHUNK
    half, quarter = C // 2, C // 4
    piece = N // F
    n = piece // C
    L1, L3, L4, L5 = LAGS
    (design, passive, state, adjoint, dq, dlo, dhi, nd, nrecv, nbuf, rowed, tmp, filt, own, factor,
     tq, tsc, trecv, tsr, sq, ssc, slo, slos, shi, shis, gq, gsc, grecv, gsr, joined, part, parts,
     in_sem, d_s, d_r, n_s, n_r, t_s, t_r, s_s, s_r, g_s, g_r, p_s, p_r) = scratch
    r = lax.axis_index("rows")
    me = lax.axis_index("freq")
    has_lo = r > 0
    has_hi = r < R - 1
    below_id = {"rows": jnp.maximum(r - 1, 0)}
    above_id = {"rows": jnp.minimum(r + 1, R - 1)}

    def loads(k):
        copies = []
        for p in range(F):
            g = p * n + k
            cols = ds(g * C, C)
            copies += [
                pltpu.make_async_copy(design_h.at[:, cols], design.at[:, cols], in_sem.at[0, g]),
                pltpu.make_async_copy(state_h.at[:, :, :, cols], state.at[:, :, :, cols], in_sem.at[1, g]),
                pltpu.make_async_copy(adjoint_h.at[:, :, :, cols], adjoint.at[:, :, :, cols], in_sem.at[2, g]),
                pltpu.make_async_copy(passive_h.at[:, cols], passive.at[:, cols], in_sem.at[3, g]),
            ]
        return copies

    def begin(k, c):
        for copy in loads(k):
            copy.start()
        return c

    lax.fori_loop(0, n, begin, 0)

    bar = pltpu.get_barrier_semaphore()
    for d in range(1, R):
        pl.semaphore_signal(bar, inc=1, device_id={"rows": lax.rem(r + d, R)}, device_id_type=MESH)
    for d in range(1, F):
        pl.semaphore_signal(bar, inc=1, device_id={"freq": lax.rem(me + d, F)}, device_id_type=MESH)

    edge = jnp.zeros((8, 128), jnp.float32)
    for buf in (rowed, joined):
        buf[:, pl.ds(0, 128)] = edge
        buf[:, pl.ds(N + 128, 128)] = edge
    for buf in (state, adjoint):
        for j in range(2):
            for s in range(S):
                buf[j, s, :, pl.ds(N, 128)] = edge.astype(jnp.bfloat16)
    nbuf[:, pl.ds(N, 128)] = jnp.zeros((nbuf.shape[0], 128), jnp.float32)

    @pl.when(jnp.logical_not(has_lo))
    def _():
        def fill(g, c):
            dlo[g] = jnp.zeros((16, half), jnp.int16)
            return c

        lax.fori_loop(0, F * n, fill, 0)

        def fill2(g, c):
            slo[g] = jnp.zeros((16, half), jnp.int16)
            slos[g] = edge
            return c

        lax.fori_loop(0, n, fill2, 0)

    @pl.when(jnp.logical_not(has_hi))
    def _():
        def fill(g, c):
            dhi[g] = jnp.zeros((16, half), jnp.int16)
            for s in range(S):
                nrecv[g, s] = jnp.zeros((16, quarter), jnp.bfloat16)
            return c

        lax.fori_loop(0, F * n, fill, 0)

        def fill2(g, c):
            shi[g] = jnp.zeros((16, half), jnp.int16)
            shis[g] = edge
            return c

        lax.fori_loop(0, n, fill2, 0)

    lo_on = has_lo.astype(jnp.float32)
    hi_on = has_hi.astype(jnp.float32)
    row = lax.broadcasted_iota(jnp.int32, (8, 128), 0)
    place = (r * 8 + row).astype(jnp.float32)
    row_inv = 1.0 / (81.0 - edge_gap(place) - edge_gap(float(R * 8 - 1) - place))
    omegas = []
    for s in range(S):
        picked = jnp.float32(0.0)
        for t in range(omega_sq.shape[0]):
            picked = picked + jnp.where(assign[s] == t, omega_sq[t], 0.0)
        omegas.append(picked)

    def remote(src, dst, send, recv, device):
        return pltpu.make_async_remote_copy(
            src_ref=src, dst_ref=dst, send_sem=send, recv_sem=recv, device_id=device, device_id_type=MESH
        )

    def d_up(g):
        return remote(dq.at[g], dlo.at[g], d_s.at[0, g], d_r.at[0, g], above_id)

    def d_down(g):
        return remote(dq.at[g], dhi.at[g], d_s.at[1, g], d_r.at[1, g], below_id)

    def n_down(g):
        return remote(nd.at[g], nrecv.at[g], n_s.at[g], n_r.at[g], below_id)

    def t_copies(d, q):
        to = {"freq": lax.rem(me + d, F)}
        return (
            remote(tq.at[d - 1, q], trecv.at[d - 1, q], t_s.at[0, d - 1, q], t_r.at[0, d - 1, q], to),
            remote(tsc.at[d - 1, q], tsr.at[d - 1, q], t_s.at[1, d - 1, q], t_r.at[1, d - 1, q], to),
        )

    def s_up(q):
        return (
            remote(sq.at[q], slo.at[q], s_s.at[0, q], s_r.at[0, q], above_id),
            remote(ssc.at[q], slos.at[q], s_s.at[1, q], s_r.at[1, q], above_id),
        )

    def s_down(q):
        return (
            remote(sq.at[q], shi.at[q], s_s.at[2, q], s_r.at[2, q], below_id),
            remote(ssc.at[q], shis.at[q], s_s.at[3, q], s_r.at[3, q], below_id),
        )

    def g_copies(d, q):
        to = {"freq": lax.rem(me + d, F)}
        return (
            remote(gq.at[q], grecv.at[d - 1, q], g_s.at[0, d - 1, q], g_r.at[0, d - 1, q], to),
            remote(gsc.at[q], gsr.at[d - 1, q], g_s.at[1, d - 1, q], g_r.at[1, d - 1, q], to),
        )

    def encode(load, code_ref, scale_ref):
        acc = None
        for b in range(C // SUB):
            tile = peak([load(b * SUB, SUB)])
            acc = tile if acc is None else jnp.maximum(acc, tile)
        fine = acc > 1e-30
        scale_ref[...] = jnp.where(fine, acc * (1.0 / BIG), 0.0)
        inv = wide(jnp.where(fine, BIG / jnp.where(fine, acc, 1.0), 0.0), SUB)
        for b in range(half // SUB):
            code_ref[:, pl.ds(b * SUB, SUB)] = to_code(
                load(b * SUB, SUB) * inv, load(half + b * SUB, SUB) * inv
            )

    def stage0(k):
        for copy in loads(k):
            copy.wait()
        for p in range(F):
            g = p * n + k
            col = g * C
            for b in range(half // SUB):
                x0 = design[:, ds(col + b * SUB, SUB)]
                x1 = design[:, ds(col + half + b * SUB, SUB)]
                dq[g, :, pl.ds(b * SUB, SUB)] = to_code((x0 - 0.5) * 65536.0, (x1 - 0.5) * 65536.0)
            rows16 = lax.broadcasted_iota(jnp.int32, (8, quarter), 0)
            for s in range(S):
                packs = []
                for src in (state, adjoint):
                    acc = jnp.zeros((8, quarter), jnp.float32)
                    for j in range(2):
                        x = src[j, s, :, ds(col, C)].astype(jnp.float32)[0:1]
                        for b in range(4):
                            line = jnp.broadcast_to(x[:, b * quarter : (b + 1) * quarter], (8, quarter))
                            acc = jnp.where(rows16 == j * 4 + b, line, acc)
                    packs.append(acc)
                nd[g, s] = jnp.concatenate(packs, axis=0).astype(jnp.bfloat16)

    def send0(k):
        for p in range(F):
            g = p * n + k

            @pl.when(has_hi)
            def _():
                d_up(g).start()

            @pl.when(has_lo)
            def _():
                d_down(g).start()
                n_down(g).start()

    def stage1(k):
        for p in range(F):
            g = p * n + k
            col = g * C

            @pl.when(has_lo)
            def _():
                d_up(g).wait_recv()

            @pl.when(has_hi)
            def _():
                d_down(g).wait_recv()
                n_down(g).wait_recv()

            for s in range(S):
                rows16 = nrecv[g, s].astype(jnp.float32)
                for t in range(4):
                    for b in range(4):
                        nbuf[pl.ds(s * 8 + t, 1), ds(col + b * quarter, quarter)] = rows16[
                            t * 4 + b : t * 4 + b + 1
                        ]
            for b in range(half // SUB):
                lows = from_code(dlo[g, :, pl.ds(b * SUB, SUB)])
                highs = from_code(dhi[g, :, pl.ds(b * SUB, SUB)])
                for h in range(2):
                    at = col + h * half + b * SUB
                    low = (lows[h] * (1.0 / 65536.0) + 0.5) * lo_on
                    high = (highs[h] * (1.0 / 65536.0) + 0.5) * hi_on
                    rowed[:, ds(at + 128, SUB)] = row_taps(low, design[:, ds(at, SUB)], high)

    row_sub = lax.broadcasted_iota(jnp.int32, (8, TSUB + 128), 0)

    def haar(src, j, s, t, at):
        x = src[j, s, :, ds(at, TSUB + 128)].astype(jnp.float32)
        next_line = nbuf[pl.ds(s * 8 + t, 1), ds(at, TSUB + 128)]
        below = jnp.where(row_sub == 7, next_line, pltpu.roll(x, 7, 0))
        out = []
        for y in (x + below, x - below):
            right = pltpu.roll(y, TSUB + 127, 1)[:, :TSUB]
            y = y[:, :TSUB]
            out.extend((y + right, y - right))
        return out

    def terms(at, o):
        j = (at + lax.broadcasted_iota(jnp.int32, (1, TSUB), 1)).astype(jnp.float32)
        col_inv = 1.0 / (81.0 - edge_gap(j) - edge_gap(float(N - 1) - j))
        weight = wide(row_inv, TSUB) * col_inv
        tilde = filt[:, ds(o, TSUB)] * weight
        top = jnp.tanh(jnp.full((8, TSUB), SHARP * 0.5, jnp.float32))
        inv_q = 0.5 / top
        t = jnp.tanh(SHARP * (tilde - 0.5))
        solid = passive[:, ds(at, TSUB)] > 0
        density = jnp.where(solid, 1.0, (top + t) * inv_q)
        slope = jnp.where(solid, 0.0, SHARP * (1.0 - t * t) * inv_q)
        stiff = 3.0 * density * density * (1.0 - 0.001)
        total = None
        for s in range(S):
            sr = haar(state, 0, s, 0, at)
            si = haar(state, 1, s, 1, at)
            ar = haar(adjoint, 0, s, 2, at)
            ai = haar(adjoint, 1, s, 3, at)
            direct = [ar[c] * sr[c] - ai[c] * si[c] for c in range(4)]
            cross = [ar[c] * si[c] + ai[c] * sr[c] for c in range(1, 4)]
            mix = [None] + [direct[c] - 0.2 * cross[c - 1] for c in range(1, 4)]
            stiffly = 0.25 * (mix[1] + mix[2]) + (1.0 / 6.0) * mix[3]
            mass = (1.0 / 16.0) * direct[0] + (1.0 / 48.0) * (direct[1] + direct[2]) + (1.0 / 144.0) * direct[3]
            value = stiff * stiffly - omegas[s] * mass
            total = value if total is None else total + value
        return total, slope * weight

    def filtered(col):
        def body(b, c):
            filt[:, ds(b * CSUB, CSUB)] = col_taps(rowed[:, ds(col + b * CSUB, CSUB + 256)])
            return c

        lax.fori_loop(0, C // CSUB, body, 0, unroll=CUN)

    def stage2(q):
        for d in range(1, F):
            col = (lax.rem(me + d, F) * n + q) * C

            filtered(col)

            def body(b, c):
                value, unused = terms(col + b * TSUB, b * TSUB)
                tmp[:, ds(b * TSUB, TSUB)] = value
                return c

            lax.fori_loop(0, C // TSUB, body, 0, unroll=TUN)
            encode(lambda o, w: tmp[:, pl.ds(o, w)], tq.at[d - 1, q], tsc.at[d - 1, q])
        col = (me * n + q) * C

        filtered(col)

        def body(b, c):
            value, slope = terms(col + b * TSUB, b * TSUB)
            own[:, ds(q * C + b * TSUB, TSUB)] = value
            factor[:, ds(q * C + b * TSUB, TSUB)] = slope
            return c

        lax.fori_loop(0, C // TSUB, body, 0, unroll=TUN)
        for d in range(1, F):
            for copy in t_copies(d, q):
                copy.start()

    def stage3(q):
        for d in range(1, F):
            for copy in t_copies(d, q):
                copy.wait_recv()
        for b in range(half // SUB):
            sums = [own[:, ds(q * C + h * half + b * SUB, SUB)] for h in range(2)]
            for d in range(1, F):
                got = from_code(trecv[d - 1, q, :, pl.ds(b * SUB, SUB)])
                scale = wide(tsr[d - 1, q], SUB)
                sums = [sums[h] + got[h] * scale for h in range(2)]
            for h in range(2):
                at = q * C + h * half + b * SUB
                own[:, ds(at, SUB)] = sums[h] * factor[:, ds(at, SUB)]
        encode(lambda o, w: own[:, ds(q * C + o, w)], sq.at[q], ssc.at[q])

    def send3(q):
        @pl.when(has_hi)
        def _():
            for copy in s_up(q):
                copy.start()

        @pl.when(has_lo)
        def _():
            for copy in s_down(q):
                copy.start()

    def stage4(q):
        @pl.when(has_lo)
        def _():
            for copy in s_up(q):
                copy.wait_recv()

        @pl.when(has_hi)
        def _():
            for copy in s_down(q):
                copy.wait_recv()

        base = (me * n + q) * C + 128
        for b in range(half // SUB):
            lows = from_code(slo[q, :, pl.ds(b * SUB, SUB)])
            highs = from_code(shi[q, :, pl.ds(b * SUB, SUB)])
            los, his = wide(slos[q], SUB), wide(shis[q], SUB)
            for h in range(2):
                at = h * half + b * SUB
                joined[:, ds(base + at, SUB)] = row_taps(
                    lows[h] * los, own[:, ds(q * C + at, SUB)], highs[h] * his
                )
        encode(lambda o, w: joined[:, ds(base + o, w)], gq.at[q], gsc.at[q])

    def send4(q):
        for d in range(1, F):
            for copy in g_copies(d, q):
                copy.start()

    def stage5(q):
        for d in range(1, F):
            for copy in g_copies(d, q):
                copy.wait_recv()
            base = (lax.rem(me + F - d, F) * n + q) * C + 128
            scale = wide(gsr[d - 1, q], SUB)
            for b in range(half // SUB):
                got = from_code(grecv[d - 1, q, :, pl.ds(b * SUB, SUB)])
                for h in range(2):
                    joined[:, ds(base + h * half + b * SUB, SUB)] = got[h] * scale

    def stage6(q):
        for p in range(F):
            col = (p * n + q) * C

            def body(b, acc):
                at = col + b * CSUB
                value = col_taps(joined[:, ds(at, CSUB + 256)])
                back_o[:, ds(at, CSUB)] = value
                for t in range(CSUB // 128):
                    tile = value[:, t * 128 : (t + 1) * 128]
                    acc = acc + tile * tile
                return acc

            part[...] = lax.fori_loop(0, C // CSUB, body, part[...], unroll=CUN)

    part[...] = edge
    pl.semaphore_wait(bar, R - 1 + F - 1)

    o1 = L1
    o2 = o1 + 2
    o3 = o2 + L3
    o4 = o3 + L4
    o5 = o4 + L5
    o6 = o5 + 2

    def guarded(fn, it, offset, turn):
        i = it - offset
        arg = lax.rem(i + turn + n, n)

        @pl.when((i >= 0) & (i < n))
        def _():
            fn(arg)

    def step(it, carry):
        guarded(stage0, it, 0, 0)
        guarded(stage3, it, o3, 1)
        guarded(send0, it, 0, 0)
        guarded(stage4, it, o4, 1)
        guarded(send3, it, o3, 1)
        guarded(stage1, it, o1, 0)
        guarded(send4, it, o4, 1)
        guarded(stage2, it, o2, 1)
        guarded(stage5, it, o5, 1)
        guarded(stage6, it, o6, 2)
        return carry

    lax.fori_loop(0, n + o6, step, 0)

    def send_waits(k, c):
        for p in range(F):
            g = p * n + k

            @pl.when(has_hi)
            def _():
                d_up(g).wait_send()

            @pl.when(has_lo)
            def _():
                d_down(g).wait_send()
                n_down(g).wait_send()

        for d in range(1, F):
            for copy in t_copies(d, k) + g_copies(d, k):
                copy.wait_send()

        @pl.when(has_hi)
        def _():
            for copy in s_up(k):
                copy.wait_send()

        @pl.when(has_lo)
        def _():
            for copy in s_down(k):
                copy.wait_send()

        return c

    lax.fori_loop(0, n, send_waits, 0)

    def sum_copy(d):
        return remote(part, parts.at[d - 1], p_s.at[d - 1], p_r.at[d - 1], {"rows": lax.rem(r + d, R)})

    for d in range(1, R):
        sum_copy(d).start()
    acc = part[...]
    for d in range(1, R):
        sum_copy(d).wait_recv()
        acc = acc + parts[d - 1]
    total = jnp.sum(acc, keepdims=True)
    inverse = lax.rsqrt(jnp.broadcast_to(total, (8, 128)) / float(R * 8 * N) + EPSILON)
    scale_o[0, 0] = jnp.max(inverse)
    for d in range(1, R):
        sum_copy(d).wait_send()


def shards(sizes, design, passive, state, adjoint, omega_sq, assign):
    R, F, N, S = sizes
    C = CHUNK
    half, quarter = C // 2, C // 4
    piece = N // F
    n = piece // C
    G = F * n
    f32, i16, bf16 = jnp.float32, jnp.int16, jnp.bfloat16
    V = pltpu.VMEM
    dma = pltpu.SemaphoreType.DMA
    scratch = [
        V((8, N), f32), V((8, N), jnp.int32), V((2, S, 8, N + 128), bf16), V((2, S, 8, N + 128), bf16),
        V((G, 16, half), i16), V((G, 16, half), i16), V((G, 16, half), i16),
        V((G, S, 16, quarter), bf16), V((G, S, 16, quarter), bf16), V((8 * S, N + 128), f32),
        V((8, N + 256), f32), V((8, C), f32), V((8, C), f32), V((8, piece), f32), V((8, piece), f32),
        V((F - 1, n, 16, half), i16), V((F - 1, n, 8, 128), f32),
        V((F - 1, n, 16, half), i16), V((F - 1, n, 8, 128), f32),
        V((n, 16, half), i16), V((n, 8, 128), f32),
        V((n, 16, half), i16), V((n, 8, 128), f32), V((n, 16, half), i16), V((n, 8, 128), f32),
        V((n, 16, half), i16), V((n, 8, 128), f32),
        V((F - 1, n, 16, half), i16), V((F - 1, n, 8, 128), f32),
        V((8, N + 256), f32), V((8, 128), f32), V((R - 1, 8, 128), f32),
        dma((4, G)), dma((2, G)), dma((2, G)), dma((G,)), dma((G,)),
        dma((2, F - 1, n)), dma((2, F - 1, n)), dma((4, n)), dma((4, n)),
        dma((2, F - 1, n)), dma((2, F - 1, n)), dma((R - 1,)), dma((R - 1,)),
    ]
    anywhere = pl.BlockSpec(memory_space=pl.ANY)
    small = pl.BlockSpec(memory_space=pltpu.SMEM)
    vmem = pl.BlockSpec(memory_space=pltpu.VMEM)
    back, scale = pl.pallas_call(
        functools.partial(kernel, sizes),
        out_shape=(jax.ShapeDtypeStruct((8, N), f32), jax.ShapeDtypeStruct((1, 1), f32)),
        in_specs=[anywhere] * 4 + [small] * 2,
        out_specs=(vmem, small),
        scratch_shapes=scratch,
        compiler_params=pltpu.CompilerParams(
            collective_id=0, has_side_effects=True, vmem_limit_bytes=60 * 1024 * 1024
        ),
    )(design, passive, state, adjoint, omega_sq, assign)
    return back * scale


def solution(mesh):
    R, F = mesh.shape["rows"], mesh.shape["freq"]

    def run(design, passive, state, adjoint, omega_sq, assign):
        sizes = (R, F, design.shape[1], state.shape[1])
        return shards(sizes, design, passive, state, adjoint, omega_sq, assign)

    return jax.shard_map(
        run,
        mesh=mesh,
        in_specs=(
            P("rows", None),
            P("rows", None),
            P(None, "freq", "rows", None),
            P(None, "freq", "rows", None),
            P(),
            P("freq"),
        ),
        out_specs=P("rows", None),
        check_vma=False,
    )
```
